32 devices in a mesh: grp: 2 (over y), blk: 4 (over z), sub: 2 (over x), frq: 2 (over core).
Axes of the slice: x: 2, y: 2, z: 4, core: 2. Of those that a mesh axis runs over, the one named last changes fastest.
Arguments:
- spectra: bfloat16 [2, 8192, 4096], P(None, ('grp', 'blk'), ('sub', 'frq')), parts along dimension 1, may hold values from -6 to 6
- channel_mask: int32 [8, 1024], P(('grp', 'blk')), parts along dimension 0, may hold values 0 or 1
- local_channel: int32 [8, 4, 48], P(('grp', 'blk')), parts along dimension 0, may hold values from 0 to 1023
- partner_channel: int32 [8, 4, 48], P(('grp', 'blk')), parts along dimension 0, may hold values from 0 to 31
- stack_owner: int32 [8, 4, 48, 1], P(('grp', 'blk')), parts along dimension 0, may hold values from 0 to 3; in each aligned block of 192 rows (0 to 191, 192 to 383, ..., all dimensions but the last counted through in order) at most 96 rows name the same one
- stack_slot: int32 [8, 4, 48], P(('grp', 'blk')), parts along dimension 0, may hold values from 0 to 31
Outputs:
- stacks: float32 [256, 1024], P(('grp', 'blk'), ('sub', 'frq')), parts along dimension 0
The draws below stay inside these ranges and needn't reach their ends.
There are 2 independent parts, one for each index of `grp`. The reference program is written for one: setup_inputs(seed, part) draws one part's arguments, and reference() takes and returns one part's arrays. A program takes and returns all parts, laid end to end along the dimension named above; each array names one. Nothing has to cross between parts.
Inputs may be any that keep to these rules, and one draw needn't show every extreme that they name: `stack_owner`: of the pairs of one source block, at most 96 name one owner, a bound that some block reaches of them.
All inputs are finite; a program needn't handle non-finite values. No bound on the sum of `channel_mask` on one device may be relied on, other than what follows from the above.
Results may differ from the reference program's by a relative error of at most 0.009.
Values may be sent and summed in bfloat16 or wider, within the bound.
A program may use at most 64 MiB of HBM per device.

```python
import math
import jax
import jax.numpy as jnp
import numpy as np
from jax import lax

NF = 4096
LAGS = 1024
CH_BLK = 1024
VS_BLK = 32
PS = 48
SLOTS_DEV = 32
CAP = 96
FGROUPS = 4
FBINS = 1024
CHANNELS = 4096
SLOTS = 128
N_BLK = 4


def plant(array, rng, low, largest):
    longest = array.shape.index(max(array.shape))
    spots = []
    for shift in (0, 1):
        where = [jax.random.randint(jax.random.fold_in(rng, axis), (), 0, length) for axis, length in enumerate(array.shape)]
        where[longest] = (where[longest] + shift) % array.shape[longest]
        spots.append(tuple(where))
    return array.at[spots[0]].set(low).at[spots[1]].set(largest)


def block_scale(stream_key, shape, cuts, smallest, largest):
    level = 1.0
    for dim, shards_of in cuts:
        draws = jax.random.uniform(jax.random.fold_in(jax.random.fold_in(stream_key, 6), dim), (shards_of,), jnp.float32, smallest / len(cuts), largest / len(cuts))
        level = level * jnp.repeat(jnp.exp(draws), shape[dim] // shards_of).reshape((-1,) + (1,) * (len(shape) - 1 - dim))
    return level


def routed_block(key, own, number, rows, amount, top, limit, lean):
    order = jax.random.permutation(key, amount)
    packed, common = load_shares(amount, rows * top, limit, lean, True), load_shares(amount, rows * top, limit, lean, False)
    places = jnp.arange(amount)

    def named(sizes, turn):
        used = int((sizes > 0).sum())
        fixed = max(1, used // 4)
        passed = fixed + (places - fixed + turn * (used - fixed)) % max(1, amount - fixed)
        return jnp.zeros((amount,), jnp.int32).at[order[jnp.where(places < fixed, places, passed)]].set(jnp.asarray(sizes, jnp.int32))

    sizes = jnp.where(number % 4 == 0, named(packed, number // 4), named(common, number - number // 4 - 1))
    mixed = jax.random.permutation(jax.random.fold_in(own, 3), amount)
    donor, taker = mixed[0:amount // 2 * 2:2], mixed[1:amount // 2 * 2:2]
    room = jnp.minimum(sizes[donor] - 1, limit - sizes[taker]) // 2
    room = jnp.where((donor == order[0]) | (taker == order[0]) | (sizes[taker] == 0), 0, jnp.maximum(room, 0))
    passed = jax.random.randint(jax.random.fold_in(own, 4), (amount // 2,), 0, 1 << 20) % (room + 1)
    sizes = sizes.at[donor].add(-passed).at[taker].add(passed)
    labels = jnp.searchsorted(jnp.cumsum(sizes), jnp.arange(rows * top), side="right").astype(jnp.int32)
    listing = labels.reshape(top, rows).T
    listing = listing[jax.random.permutation(jax.random.fold_in(own, 1), rows)]
    turn = jax.random.randint(jax.random.fold_in(own, 2), (rows, 1), 0, top)
    return jnp.take_along_axis(listing, (jnp.arange(top)[None, :] + turn) % top, axis=1)


def load_shares(amount, total, bound, slope, full):
    weights = [(1 << 20) // math.isqrt(rank ** slope) + 1 for rank in range(1, amount + 1)]
    largest = bound if full else min(bound, max(-(-total // amount), total * weights[0] // sum(weights)))
    least = 1 if total - largest >= amount - 1 else 0
    holding, rest = [largest] + [least] * (amount - 1), total - largest - least * (amount - 1)
    while rest > 0:
        free = [i for i in range(1, amount) if holding[i] < largest] or [i for i in range(1, amount) if holding[i] < bound]
        pool, budget = sum([weights[i] for i in free]), rest
        for i in free:
            extra = min(bound - holding[i], max(1, budget * weights[i] // pool), rest)
            holding[i] = holding[i] + extra
            rest = rest - extra
    return np.array(holding)


def normal_values(rng, extent, spread, bound, split=(), kind=jnp.bfloat16):
    level = block_scale(rng, extent, split, -0.22, 0.18) if split else 1.0
    array = jax.random.normal(rng, extent, jnp.float32) * spread * level
    return jnp.minimum(jnp.maximum(array, -bound), bound).astype(kind)


def setup_inputs(seed: int = 0, part: int = 0) -> dict:
    splits = jax.random.split(jax.random.key(seed), 7)
    part_keys = jax.random.split(jax.random.fold_in(splits[6], part), 7)
    spectra = normal_values(part_keys[0], (2, CHANNELS, NF), 1.0, 6.0, ((1, 4), (2, 4)))
    channel_mask = plant((jax.random.randint(part_keys[1], (N_BLK, CH_BLK), 0, 8) < 7).astype(jnp.int32), jax.random.fold_in(part_keys[1], 1), 0, 1)
    local_channel = plant(jax.random.randint(part_keys[2], (N_BLK, N_BLK, PS), 0, CH_BLK), jax.random.fold_in(part_keys[2], 1), 0, CH_BLK - 1).astype(jnp.int32)
    partner_channel = plant(jax.random.randint(part_keys[3], (N_BLK, N_BLK, PS), 0, VS_BLK), jax.random.fold_in(part_keys[3], 1), 0, VS_BLK - 1).astype(jnp.int32)
    stack_owner_keys = jax.random.split(jax.random.fold_in(part_keys[4], 1), N_BLK * N_BLK * PS // (N_BLK * PS))
    stack_owner_turns = jax.random.permutation(jax.random.fold_in(part_keys[4], 3), N_BLK * N_BLK * PS // (N_BLK * PS))
    stack_owner = jax.vmap(lambda own, number: routed_block(jax.random.fold_in(part_keys[4], 2), own, number, N_BLK * PS, N_BLK, 1, CAP, 2))(stack_owner_keys, stack_owner_turns).reshape((N_BLK, N_BLK, PS, 1))
    stack_slot = plant(jax.random.randint(part_keys[5], (N_BLK, N_BLK, PS), 0, SLOTS_DEV), jax.random.fold_in(part_keys[5], 1), 0, SLOTS_DEV - 1).astype(jnp.int32)
    return {"spectra": spectra, "channel_mask": channel_mask, "local_channel": local_channel, "partner_channel": partner_channel, "stack_owner": stack_owner, "stack_slot": stack_slot}


def lag_rows(first_bin, bin_count):
    bin_index = first_bin + jnp.arange(bin_count, dtype=jnp.int32)
    shifts = jnp.arange(LAGS, dtype=jnp.int32) - LAGS // 2
    phase_angle = jnp.mod(bin_index[:, None] * shifts[None, :], NF).astype(jnp.float32) * (2.0 * math.pi / NF)
    factor = 1.0 / math.sqrt(NF)
    return jnp.concatenate([jnp.cos(phase_angle) * factor, -jnp.sin(phase_angle) * factor], axis=0).astype(jnp.bfloat16)

def reference(spectra, channel_mask, local_channel, partner_channel, stack_owner, stack_slot):
    masked = spectra * channel_mask.reshape(-1).astype(jnp.bfloat16)[None, :, None]
    tables = [lag_rows(group_index * FBINS, FBINS) for group_index in range(FGROUPS)]
    panel_base = (jnp.arange(N_BLK, dtype=jnp.int32) * CH_BLK)[:, None]
    stride_size = CH_BLK // VS_BLK

    def block_pairs(source):
        own_index = (source * CH_BLK + local_channel[source]).reshape(-1).astype(jnp.int32)
        partner_index = (panel_base + partner_channel[source] * stride_size).reshape(-1).astype(jnp.int32)
        own_spectra = jnp.take(masked, own_index, axis=1).astype(jnp.float32)
        partner_spectra = jnp.take(masked, partner_index, axis=1).astype(jnp.float32)
        real_part = (own_spectra[0] * partner_spectra[0] + own_spectra[1] * partner_spectra[1]).astype(jnp.bfloat16)
        imag_part = (own_spectra[1] * partner_spectra[0] - own_spectra[0] * partner_spectra[1]).astype(jnp.bfloat16)
        running_sum = jnp.zeros((own_index.shape[0], LAGS), jnp.float32)
        for group_index in range(FGROUPS):
            first_bin = group_index * FBINS
            last_bin = first_bin + FBINS
            cross_rows = jnp.concatenate([real_part[:, first_bin:last_bin], imag_part[:, first_bin:last_bin]], axis=1)
            partial_value = jnp.dot(cross_rows, tables[group_index], preferred_element_type=jnp.float32).astype(jnp.bfloat16)
            running_sum = running_sum + lax.optimization_barrier(partial_value).astype(jnp.float32)
        return running_sum.astype(jnp.bfloat16)
    correlation = lax.map(block_pairs, jnp.arange(N_BLK, dtype=jnp.int32))
    stack_rows = (stack_owner[..., 0] * SLOTS_DEV + stack_slot).reshape(-1).astype(jnp.int32)
    flat_corr = lax.optimization_barrier(correlation).reshape(-1, LAGS).astype(jnp.float32)
    return jax.ops.segment_sum(flat_corr, stack_rows, num_segments=SLOTS)
```

```python
import functools
import math

import jax
import jax.numpy as jnp
import numpy as np
from jax import lax
from jax.experimental import pallas as pl
from jax.experimental.pallas import tpu as pltpu
from jax.sharding import PartitionSpec as P

NF = 4096
LAGS = 1024
VS_BLK = 32
SLOTS_DEV = 32
STEP = 32
MESH = pl.DeviceIdType.MESH


def phase_rows(bins):
    shifts = np.arange(LAGS, dtype=np.int64) - LAGS // 2
    angle = np.mod(bins[:, None] * shifts[None, :], NF) * (2.0 * math.pi / NF)
    return np.stack([np.cos(angle), -np.sin(angle)])


def loop(count, body):
    if count == 1:
        body(0)
    else:
        lax.fori_loop(0, count, lambda i, carry: (body(i), carry)[1], 0)


def kernel(n, nsub, nfrq, chunks, pair_block, stack_block,
           spectra, mask_ref, cols_ref, rows_ref, coarse, fine_ref, out_ref,
           spec, tiles, panels, own, hot, sel, cross, stacked, table, coarse_v, acc,
           send1, recv1, total, send2, recv2,
           load_sem, right_send, right_recv, left_send, left_recv,
           s1_send, s1_recv, s2_send, s2_recv):
    z = lax.axis_index("blk")
    sub, frq = lax.axis_index("sub"), lax.axis_index("frq")
    place = sub * nfrq + frq
    channels, bins = spec.shape[1], spec.shape[2]
    width = bins // chunks
    pairs, stacks = own.shape[1], acc.shape[0]
    lag_width = out_ref.shape[1]
    coarse_rows = bins // STEP
    peers = [(ds, df) for ds in range(nsub - 1, -1, -1) for df in range(nfrq - 1, -1, -1)]

    tile_load = pltpu.make_async_copy(spectra.at[:, :, pl.ds(0, 8), :], tiles, load_sem.at[0])
    tile_load.start()
    flat = spectra.reshape(2, channels, bins)
    spec_loads = []
    for c in range(chunks):
        lanes = pl.ds(c * width, width)
        spec_loads.append(pltpu.make_async_copy(
            flat.at[:, :, lanes], spec.at[:, :, lanes], load_sem.at[2 + c]))
    coarse_load = pltpu.make_async_copy(
        coarse.at[:, pl.ds(pl.multiple_of(place * coarse_rows, 8), coarse_rows), :],
        coarse_v, load_sem.at[1])
    for load in spec_loads:
        load.start()
    coarse_load.start()

    barrier = pltpu.get_barrier_semaphore()
    for k in range(1, n):
        pl.semaphore_signal(barrier, inc=1, device_id={"blk": lax.rem(z + k, n)}, device_id_type=MESH)
    for ds, df in peers[:-1]:
        pl.semaphore_signal(
            barrier, inc=1,
            device_id={"sub": lax.rem(sub + ds, nsub), "frq": lax.rem(frq + df, nfrq)},
            device_id_type=MESH)

    mask = mask_ref[...]
    at_row = lax.broadcasted_iota(jnp.int32, (VS_BLK, channels), 0)
    at_lane = lax.broadcasted_iota(jnp.int32, (VS_BLK, channels), 1)
    source_mask = jnp.sum(
        jnp.where(at_lane == at_row * (channels // VS_BLK), mask, 0).astype(jnp.float32),
        axis=1, keepdims=True)
    pick_row = lax.broadcasted_iota(jnp.int32, (VS_BLK, 8 * VS_BLK), 0)
    pick_lane = lax.broadcasted_iota(jnp.int32, (VS_BLK, 8 * VS_BLK), 1)
    pick = jnp.where(pick_lane == 8 * pick_row, source_mask, 0.0).astype(jnp.bfloat16)
    tile_load.wait()
    for part in range(2):
        picked = jnp.dot(pick, tiles[part].reshape(8 * VS_BLK, bins),
                         preferred_element_type=jnp.float32).astype(jnp.bfloat16)
        for c in range(chunks):
            panels[z, c, part] = picked[:, c * width:(c + 1) * width]
    pl.semaphore_wait(barrier, n - 1 + len(peers) - 1)

    def to_right(c, d):
        return pltpu.make_async_remote_copy(
            src_ref=panels.at[z - d, c], dst_ref=panels.at[z - d, c],
            send_sem=right_send.at[c, d], recv_sem=right_recv.at[c, d],
            device_id={"blk": z + 1}, device_id_type=MESH)

    def to_left(c, d):
        return pltpu.make_async_remote_copy(
            src_ref=panels.at[z + d, c], dst_ref=panels.at[z + d, c],
            send_sem=left_send.at[c, d], recv_sem=left_recv.at[c, d],
            device_id={"blk": z - 1}, device_id_type=MESH)

    def from_left(c, d):
        return pltpu.make_async_remote_copy(
            src_ref=panels.at[z - 1 - d, c], dst_ref=panels.at[z - 1 - d, c],
            send_sem=right_send.at[c, d], recv_sem=right_recv.at[c, d],
            device_id={"blk": z - 1}, device_id_type=MESH)

    def from_right(c, d):
        return pltpu.make_async_remote_copy(
            src_ref=panels.at[z + 1 + d, c], dst_ref=panels.at[z + 1 + d, c],
            send_sem=left_send.at[c, d], recv_sem=left_recv.at[c, d],
            device_id={"blk": z + 1}, device_id_type=MESH)

    def send_on(c, d):
        @pl.when((z - d >= 0) & (z + 1 < n))
        def _():
            to_right(c, d).start()

        @pl.when((z + d < n) & (z - 1 >= 0))
        def _():
            to_left(c, d).start()

    def arrive(c, d):
        @pl.when(z - 1 - d >= 0)
        def _():
            from_left(c, d).wait_recv()

        @pl.when(z + 1 + d < n)
        def _():
            from_right(c, d).wait_recv()

        if d + 1 < n - 1:
            send_on(c, d + 1)

    for c in range(chunks):
        send_on(c, 0)

    def build_hot():
        def body(r):
            rows = pl.ds(pl.multiple_of(r * pair_block, 16), pair_block)
            lane = lax.broadcasted_iota(jnp.int32, (pair_block, channels), 1)
            hit = jnp.where(lane == cols_ref[rows, 0:1], mask, 0)
            hot[rows, :] = hit.astype(jnp.float32).astype(jnp.bfloat16)
        loop(pairs // pair_block, body)

        def body_sel(r):
            rows = pl.ds(pl.multiple_of(r * stack_block, 16), stack_block)
            row = lax.broadcasted_iota(jnp.int32, (stack_block, pairs), 0) + r * stack_block
            hit = jnp.where(row == rows_ref[0:1, :], 1.0, 0.0)
            sel[rows, :] = hit.astype(jnp.bfloat16)
        loop(stacks // stack_block, body_sel)

    def gather(c):
        spec_loads[c].wait()
        for part in range(2):
            def body(r):
                rows = pl.ds(pl.multiple_of(r * pair_block, 16), pair_block)
                lanes = pl.ds(c * width, width)
                own[part, rows, lanes] = jnp.dot(
                    hot[rows, :], spec[part, :, lanes],
                    preferred_element_type=jnp.float32).astype(jnp.bfloat16)
            loop(pairs // pair_block, body)

    def make_table(c):
        if c == 0:
            coarse_load.wait()

        def body(a):
            row = pl.ds(c * (width // STEP) + a, 1)
            high_cos, high_sin = coarse_v[0, row, :], coarse_v[1, row, :]
            low_cos, low_sin = fine_ref[0], fine_ref[1]
            rows = pl.ds(pl.multiple_of(a * STEP, STEP), STEP)
            table[c, 0, rows, :] = (high_cos * low_cos - high_sin * low_sin).astype(jnp.bfloat16)
            table[c, 1, rows, :] = (high_sin * low_cos + high_cos * low_sin).astype(jnp.bfloat16)
        loop(width // STEP, body)

    work = [functools.partial(build_hot)]
    for c in range(chunks):
        work += [functools.partial(gather, c), functools.partial(make_table, c)]
    work.pop(0)()
    work.pop(0)()

    for d in range(n - 2):
        for c in range(chunks):
            arrive(c, d)
            if work:
                work.pop(0)()
    while work:
        work.pop(0)()

    def stack_chunk(c):
        lanes = pl.ds(c * width, width)
        panel = [panels[:, c, part].reshape(n * VS_BLK, width) for part in range(2)]

        def body(r):
            rows = pl.ds(pl.multiple_of(r * pair_block, 16), pair_block)
            lane = lax.broadcasted_iota(jnp.int32, (pair_block, n * VS_BLK), 1)
            hit = jnp.where(lane == cols_ref[rows, 1:2], 1.0, 0.0).astype(jnp.bfloat16)
            partner = [jnp.dot(hit, half, preferred_element_type=jnp.float32) for half in panel]
            mine = [own[part, rows, lanes].astype(jnp.float32) for part in range(2)]
            cross[rows, 0:width] = (
                mine[0] * partner[0] + mine[1] * partner[1]).astype(jnp.bfloat16)
            cross[rows, width:2 * width] = (
                mine[1] * partner[0] - mine[0] * partner[1]).astype(jnp.bfloat16)
        loop(pairs // pair_block, body)

        def body_stack(r):
            rows = pl.ds(pl.multiple_of(r * stack_block, 16), stack_block)
            stacked[rows, :] = jnp.dot(
                sel[rows, :], cross[...], preferred_element_type=jnp.float32).astype(jnp.bfloat16)
        loop(stacks // stack_block, body_stack)

    for c in range(chunks):
        arrive(c, n - 2)
        stack_chunk(c)
        if c < chunks - 1:
            def body(r):
                rows = pl.ds(pl.multiple_of(r * stack_block, 16), stack_block)
                product = jnp.dot(
                    stacked[rows, :], table[c].reshape(2 * width, LAGS),
                    preferred_element_type=jnp.float32)
                acc[rows, :] = product if c == 0 else acc[rows, :] + product
            loop(stacks // stack_block, body)

    sends1 = []
    last = chunks - 1
    for k, (ds, df) in enumerate(peers):
        to_sub, to_frq = lax.rem(sub + ds, nsub), lax.rem(frq + df, nfrq)
        lanes = pl.ds(pl.multiple_of((to_sub * nfrq + to_frq) * lag_width, 128), lag_width)
        own_share = k == len(peers) - 1

        def body(r):
            rows = pl.ds(pl.multiple_of(r * stack_block, 16), stack_block)
            product = jnp.dot(
                stacked[rows, :], table[last, :, :, lanes].reshape(2 * width, lag_width),
                preferred_element_type=jnp.float32)
            if last > 0:
                product = product + acc[rows, lanes]
            if own_share:
                total[rows, :] = product
            else:
                send1[k, rows, :] = product.astype(jnp.bfloat16)
        loop(stacks // stack_block, body)
        if not own_share:
            copy = pltpu.make_async_remote_copy(
                src_ref=send1.at[k], dst_ref=recv1.at[k],
                send_sem=s1_send.at[k], recv_sem=s1_recv.at[k],
                device_id={"sub": to_sub, "frq": to_frq}, device_id_type=MESH)
            copy.start()
            sends1.append(copy)

    for copy in sends1:
        copy.wait_recv()
    summed = total[...]
    for k in range(len(peers) - 1):
        summed = summed + recv1[k].astype(jnp.float32)
    total[...] = summed
    send2[...] = summed.astype(jnp.bfloat16).reshape(n, SLOTS_DEV, lag_width)
    sends2 = []
    for k in range(n - 1, 0, -1):
        owner = lax.rem(z + k, n)
        copy = pltpu.make_async_remote_copy(
            src_ref=send2.at[owner], dst_ref=recv2.at[k - 1],
            send_sem=s2_send.at[k - 1], recv_sem=s2_recv.at[k - 1],
            device_id={"blk": owner}, device_id_type=MESH)
        copy.start()
        sends2.append(copy)
    result = total[pl.ds(pl.multiple_of(z * SLOTS_DEV, SLOTS_DEV), SLOTS_DEV), :]

    for c in range(chunks):
        for d in range(n - 1):
            @pl.when((z - d >= 0) & (z + 1 < n))
            def _():
                to_right(c, d).wait_send()

            @pl.when((z + d < n) & (z - 1 >= 0))
            def _():
                to_left(c, d).wait_send()
    for copy in sends1:
        copy.wait_send()
    for copy in sends2:
        copy.wait_recv()
    for k in range(n - 1):
        result = result + recv2[k].astype(jnp.float32)
    out_ref[...] = result
    for copy in sends2:
        copy.wait_send()


def per_device(sizes, spectra, channel_mask, local_channel, partner_channel, stack_owner, stack_slot):
    n, nsub, nfrq = sizes
    channels, bins = spectra.shape[1], spectra.shape[2]
    chunks = 4 if n <= 8 else 1
    width = bins // chunks
    pairs = local_channel.shape[1] * local_channel.shape[2]
    stacks = n * SLOTS_DEV
    lag_width = LAGS // (nsub * nfrq)
    pair_block = 192 if pairs % 192 == 0 else pairs
    stack_block = 128 if stacks % 128 == 0 else stacks
    panel_row = partner_channel[0] + (jnp.arange(n, dtype=jnp.int32) * VS_BLK)[:, None]
    cols = jnp.stack([local_channel[0].reshape(-1), panel_row.reshape(-1)], axis=1)
    rows = (stack_owner[0, :, :, 0] * SLOTS_DEV + stack_slot[0]).reshape(1, -1)
    coarse = (phase_rows(np.arange(0, NF, STEP)) / math.sqrt(NF)).astype(np.float32)
    fine = phase_rows(np.arange(STEP)).astype(np.float32)
    bf16, f32 = jnp.bfloat16, jnp.float32
    vmem = pl.BlockSpec(memory_space=pltpu.VMEM)
    hbm = pl.BlockSpec(memory_space=pl.ANY)
    peers = nsub * nfrq
    dma = pltpu.SemaphoreType.DMA
    return pl.pallas_call(
        functools.partial(kernel, n, nsub, nfrq, chunks, pair_block, stack_block),
        out_shape=jax.ShapeDtypeStruct((SLOTS_DEV, lag_width), f32),
        in_specs=[hbm, vmem, vmem, vmem, hbm, vmem],
        out_specs=vmem,
        scratch_shapes=[
            pltpu.VMEM((2, channels, bins), bf16),
            pltpu.VMEM((2, VS_BLK, 8, bins), bf16),
            pltpu.VMEM((n, chunks, 2, VS_BLK, width), bf16),
            pltpu.VMEM((2, pairs, bins), bf16),
            pltpu.VMEM((pairs, channels), bf16),
            pltpu.VMEM((stacks, pairs), bf16),
            pltpu.VMEM((pairs, 2 * width), bf16),
            pltpu.VMEM((stacks, 2 * width), bf16),
            pltpu.VMEM((chunks, 2, width, LAGS), bf16),
            pltpu.VMEM((2, bins // STEP, LAGS), f32),
            pltpu.VMEM((stacks, LAGS), f32),
            pltpu.VMEM((peers - 1, stacks, lag_width), bf16),
            pltpu.VMEM((peers - 1, stacks, lag_width), bf16),
            pltpu.VMEM((stacks, lag_width), f32),
            pltpu.VMEM((n, SLOTS_DEV, lag_width), bf16),
            pltpu.VMEM((n - 1, SLOTS_DEV, lag_width), bf16),
            dma((2 + chunks,)),
            dma((chunks, n - 1)), dma((chunks, n - 1)),
            dma((chunks, n - 1)), dma((chunks, n - 1)),
            dma((peers - 1,)), dma((peers - 1,)),
            dma((n - 1,)), dma((n - 1,)),
        ],
        compiler_params=pltpu.CompilerParams(collective_id=0, has_side_effects=True),
    )(spectra.reshape(2, VS_BLK, channels // VS_BLK, bins), channel_mask, cols, rows,
      jnp.asarray(coarse), jnp.asarray(fine))


def solution(mesh):
    sizes = (mesh.shape["blk"], mesh.shape["sub"], mesh.shape["frq"])
    return jax.shard_map(
        functools.partial(per_device, sizes),
        mesh=mesh,
        in_specs=(
            P(None, ("grp", "blk"), ("sub", "frq")),
            P(("grp", "blk"), None),
            P(("grp", "blk"), None, None),
            P(("grp", "blk"), None, None),
            P(("grp", "blk"), None, None, None),
            P(("grp", "blk"), None, None),
        ),
        out_specs=P(("grp", "blk"), ("sub", "frq")),
        check_vma=False,
    )
```

```python
import functools
import math

import jax
import jax.numpy as jnp
import numpy as np
from jax import lax
from jax.experimental import pallas as pl
from jax.experimental.pallas import tpu as pltpu
from jax.sharding import PartitionSpec as P

NF = 4096
LAGS = 1024
VS_BLK = 32
SLOTS_DEV = 32
STEP = 32
MESH = pl.DeviceIdType.MESH


def phase_rows(bins):
    shifts = np.arange(LAGS, dtype=np.int64) - LAGS // 2
    angle = np.mod(bins[:, None] * shifts[None, :], NF) * (2.0 * math.pi / NF)
    return np.stack([np.cos(angle), -np.sin(angle)])


def loop(count, body):
    if count == 1:
        body(0)
    else:
        lax.fori_loop(0, count, lambda i, carry: (body(i), carry)[1], 0)


def kernel(n, nsub, nfrq, chunks, pair_block, stack_block,
           spectra, mask_ref, local_ref, partner_ref, owner_ref, slot_ref, coarse, fine_ref, out_ref,
           index_rows, index_cols, stack_row,
           spec, tiles, panels, own, hot, sel, cross, stacked, table, coarse_v, acc,
           send1, recv1, total, send2, recv2,
           load_sem, right_send, right_recv, left_send, left_recv,
           s1_send, s1_recv, s2_send, s2_recv):
    z = lax.axis_index("blk")
    sub, frq = lax.axis_index("sub"), lax.axis_index("frq")
    place = sub * nfrq + frq
    channels, bins = spec.shape[1], spec.shape[2]
    width = bins // chunks
    pairs, stacks = own.shape[1], acc.shape[0]
    lag_width = out_ref.shape[1]
    coarse_rows = bins // STEP
    peers = [(ds, df) for ds in range(nsub - 1, -1, -1) for df in range(nfrq - 1, -1, -1)]

    tile_load = pltpu.make_async_copy(spectra.at[:, :, pl.ds(0, 8), :], tiles, load_sem.at[0])
    tile_load.start()
    flat = spectra.reshape(2, channels, bins)
    spec_loads = []
    for c in range(chunks):
        lanes = pl.ds(c * width, width)
        spec_loads.append(pltpu.make_async_copy(
            flat.at[:, :, lanes], spec.at[:, :, lanes], load_sem.at[2 + c]))
    coarse_load = pltpu.make_async_copy(
        coarse.at[:, pl.ds(pl.multiple_of(place * coarse_rows, 8), coarse_rows), :],
        coarse_v, load_sem.at[1])
    for load in spec_loads:
        load.start()
    coarse_load.start()

    barrier = pltpu.get_barrier_semaphore()
    for k in range(1, n):
        pl.semaphore_signal(barrier, inc=1, device_id={"blk": lax.rem(z + k, n)}, device_id_type=MESH)
    for ds, df in peers[:-1]:
        pl.semaphore_signal(
            barrier, inc=1,
            device_id={"sub": lax.rem(sub + ds, nsub), "frq": lax.rem(frq + df, nfrq)},
            device_id_type=MESH)

    mask = mask_ref[...]
    at_row = lax.broadcasted_iota(jnp.int32, (VS_BLK, channels), 0)
    at_lane = lax.broadcasted_iota(jnp.int32, (VS_BLK, channels), 1)
    source_mask = jnp.sum(
        jnp.where(at_lane == at_row * (channels // VS_BLK), mask, 0).astype(jnp.float32),
        axis=1, keepdims=True)
    pick_row = lax.broadcasted_iota(jnp.int32, (VS_BLK, 8 * VS_BLK), 0)
    pick_lane = lax.broadcasted_iota(jnp.int32, (VS_BLK, 8 * VS_BLK), 1)
    pick = jnp.where(pick_lane == 8 * pick_row, source_mask, 0.0).astype(jnp.bfloat16)
    tile_load.wait()
    for part in range(2):
        picked = jnp.dot(pick, tiles[part].reshape(8 * VS_BLK, bins),
                         preferred_element_type=jnp.float32).astype(jnp.bfloat16)
        for c in range(chunks):
            panels[z, c, part] = picked[:, c * width:(c + 1) * width]
    pl.semaphore_wait(barrier, n - 1 + len(peers) - 1)

    def to_right(c, d):
        return pltpu.make_async_remote_copy(
            src_ref=panels.at[z - d, c], dst_ref=panels.at[z - d, c],
            send_sem=right_send.at[c, d], recv_sem=right_recv.at[c, d],
            device_id={"blk": z + 1}, device_id_type=MESH)

    def to_left(c, d):
        return pltpu.make_async_remote_copy(
            src_ref=panels.at[z + d, c], dst_ref=panels.at[z + d, c],
            send_sem=left_send.at[c, d], recv_sem=left_recv.at[c, d],
            device_id={"blk": z - 1}, device_id_type=MESH)

    def from_left(c, d):
        return pltpu.make_async_remote_copy(
            src_ref=panels.at[z - 1 - d, c], dst_ref=panels.at[z - 1 - d, c],
            send_sem=right_send.at[c, d], recv_sem=right_recv.at[c, d],
            device_id={"blk": z - 1}, device_id_type=MESH)

    def from_right(c, d):
        return pltpu.make_async_remote_copy(
            src_ref=panels.at[z + 1 + d, c], dst_ref=panels.at[z + 1 + d, c],
            send_sem=left_send.at[c, d], recv_sem=left_recv.at[c, d],
            device_id={"blk": z + 1}, device_id_type=MESH)

    def send_on(c, d):
        @pl.when((z - d >= 0) & (z + 1 < n))
        def _():
            to_right(c, d).start()

        @pl.when((z + d < n) & (z - 1 >= 0))
        def _():
            to_left(c, d).start()

    def arrive(c, d):
        @pl.when(z - 1 - d >= 0)
        def _():
            from_left(c, d).wait_recv()

        @pl.when(z + 1 + d < n)
        def _():
            from_right(c, d).wait_recv()

        if d + 1 < n - 1:
            send_on(c, d + 1)

    for c in range(chunks):
        send_on(c, 0)

    def build_hot():
        per_panel = local_ref.shape[2]
        index_rows[...] = jnp.zeros_like(index_rows)
        index_rows[0:n, 0:per_panel] = local_ref[0].astype(jnp.float32)
        index_rows[n:2 * n, 0:per_panel] = partner_ref[0].astype(jnp.float32)
        turned = index_rows[...].T
        for p in range(n):
            rows = pl.ds(p * per_panel, per_panel)
            index_cols[rows, 0:1] = turned[0:per_panel, p:p + 1].astype(jnp.int32)
            index_cols[rows, 1:2] = turned[0:per_panel, n + p:n + p + 1].astype(jnp.int32) + p * VS_BLK
            stack_row[0:1, p * per_panel:(p + 1) * per_panel] = (
                owner_ref[p] * SLOTS_DEV + slot_ref[0, p:p + 1, :])

        def body(r):
            rows = pl.ds(pl.multiple_of(r * pair_block, 16), pair_block)
            lane = lax.broadcasted_iota(jnp.int32, (pair_block, channels), 1)
            hit = jnp.where(lane == index_cols[rows, 0:1], mask, 0)
            hot[rows, :] = hit.astype(jnp.float32).astype(jnp.bfloat16)
        loop(pairs // pair_block, body)

        def body_sel(r):
            rows = pl.ds(pl.multiple_of(r * stack_block, 16), stack_block)
            row = lax.broadcasted_iota(jnp.int32, (stack_block, pairs), 0) + r * stack_block
            hit = jnp.where(row == stack_row[0:1, :], 1.0, 0.0)
            sel[rows, :] = hit.astype(jnp.bfloat16)
        loop(stacks // stack_block, body_sel)

    def gather(c):
        spec_loads[c].wait()
        for part in range(2):
            def body(r):
                rows = pl.ds(pl.multiple_of(r * pair_block, 16), pair_block)
                lanes = pl.ds(c * width, width)
                own[part, rows, lanes] = jnp.dot(
                    hot[rows, :], spec[part, :, lanes],
                    preferred_element_type=jnp.float32).astype(jnp.bfloat16)
            loop(pairs // pair_block, body)

    def make_table(c):
        if c == 0:
            coarse_load.wait()

        def body(a):
            row = pl.ds(c * (width // STEP) + a, 1)
            high_cos, high_sin = coarse_v[0, row, :], coarse_v[1, row, :]
            low_cos, low_sin = fine_ref[0], fine_ref[1]
            rows = pl.ds(pl.multiple_of(a * STEP, STEP), STEP)
            table[c, 0, rows, :] = (high_cos * low_cos - high_sin * low_sin).astype(jnp.bfloat16)
            table[c, 1, rows, :] = (high_sin * low_cos + high_cos * low_sin).astype(jnp.bfloat16)
        loop(width // STEP, body)

    work = [functools.partial(build_hot)]
    for c in range(chunks):
        work += [functools.partial(gather, c), functools.partial(make_table, c)]
    work.pop(0)()
    work.pop(0)()

    for d in range(n - 2):
        for c in range(chunks):
            arrive(c, d)
            if work:
                work.pop(0)()
    while work:
        work.pop(0)()

    def stack_chunk(c):
        lanes = pl.ds(c * width, width)
        panel = [panels[:, c, part].reshape(n * VS_BLK, width) for part in range(2)]

        def body(r):
            rows = pl.ds(pl.multiple_of(r * pair_block, 16), pair_block)
            lane = lax.broadcasted_iota(jnp.int32, (pair_block, n * VS_BLK), 1)
            hit = jnp.where(lane == index_cols[rows, 1:2], 1.0, 0.0).astype(jnp.bfloat16)
            partner = [jnp.dot(hit, half, preferred_element_type=jnp.float32) for half in panel]
            mine = [own[part, rows, lanes].astype(jnp.float32) for part in range(2)]
            cross[rows, 0:width] = (
                mine[0] * partner[0] + mine[1] * partner[1]).astype(jnp.bfloat16)
            cross[rows, width:2 * width] = (
                mine[1] * partner[0] - mine[0] * partner[1]).astype(jnp.bfloat16)
        loop(pairs // pair_block, body)

        def body_stack(r):
            rows = pl.ds(pl.multiple_of(r * stack_block, 16), stack_block)
            stacked[rows, :] = jnp.dot(
                sel[rows, :], cross[...], preferred_element_type=jnp.float32).astype(jnp.bfloat16)
        loop(stacks // stack_block, body_stack)

    for c in range(chunks):
        arrive(c, n - 2)
        stack_chunk(c)
        if c < chunks - 1:
            def body(r):
                rows = pl.ds(pl.multiple_of(r * stack_block, 16), stack_block)
                product = jnp.dot(
                    stacked[rows, :], table[c].reshape(2 * width, LAGS),
                    preferred_element_type=jnp.float32)
                acc[rows, :] = product if c == 0 else acc[rows, :] + product
            loop(stacks // stack_block, body)

    sends1 = []
    last = chunks - 1
    for k, (ds, df) in enumerate(peers):
        to_sub, to_frq = lax.rem(sub + ds, nsub), lax.rem(frq + df, nfrq)
        lanes = pl.ds(pl.multiple_of((to_sub * nfrq + to_frq) * lag_width, 128), lag_width)
        own_share = k == len(peers) - 1

        def body(r):
            rows = pl.ds(pl.multiple_of(r * stack_block, 16), stack_block)
            product = jnp.dot(
                stacked[rows, :], table[last, :, :, lanes].reshape(2 * width, lag_width),
                preferred_element_type=jnp.float32)
            if last > 0:
                product = product + acc[rows, lanes]
            if own_share:
                total[rows, :] = product
            else:
                send1[k, rows, :] = product.astype(jnp.bfloat16)
        loop(stacks // stack_block, body)
        if not own_share:
            copy = pltpu.make_async_remote_copy(
                src_ref=send1.at[k], dst_ref=recv1.at[k],
                send_sem=s1_send.at[k], recv_sem=s1_recv.at[k],
                device_id={"sub": to_sub, "frq": to_frq}, device_id_type=MESH)
            copy.start()
            sends1.append(copy)

    for copy in sends1:
        copy.wait_recv()
    summed = total[...]
    for k in range(len(peers) - 1):
        summed = summed + recv1[k].astype(jnp.float32)
    total[...] = summed
    send2[...] = summed.astype(jnp.bfloat16).reshape(n, SLOTS_DEV, lag_width)
    sends2 = []
    for k in range(n - 1, 0, -1):
        owner = lax.rem(z + k, n)
        copy = pltpu.make_async_remote_copy(
            src_ref=send2.at[owner], dst_ref=recv2.at[k - 1],
            send_sem=s2_send.at[k - 1], recv_sem=s2_recv.at[k - 1],
            device_id={"blk": owner}, device_id_type=MESH)
        copy.start()
        sends2.append(copy)
    result = total[pl.ds(pl.multiple_of(z * SLOTS_DEV, SLOTS_DEV), SLOTS_DEV), :]

    for c in range(chunks):
        for d in range(n - 1):
            @pl.when((z - d >= 0) & (z + 1 < n))
            def _():
                to_right(c, d).wait_send()

            @pl.when((z + d < n) & (z - 1 >= 0))
            def _():
                to_left(c, d).wait_send()
    for copy in sends1:
        copy.wait_send()
    for copy in sends2:
        copy.wait_recv()
    for k in range(n - 1):
        result = result + recv2[k].astype(jnp.float32)
    out_ref[...] = result
    for copy in sends2:
        copy.wait_send()


def per_device(sizes, spectra, channel_mask, local_channel, partner_channel, stack_owner, stack_slot):
    n, nsub, nfrq = sizes
    channels, bins = spectra.shape[1], spectra.shape[2]
    chunks = 4 if n <= 8 else 1
    width = bins // chunks
    pairs = local_channel.shape[1] * local_channel.shape[2]
    stacks = n * SLOTS_DEV
    lag_width = LAGS // (nsub * nfrq)
    pair_block = 192 if pairs % 192 == 0 else pairs
    stack_block = 128 if stacks % 128 == 0 else stacks
    coarse = (phase_rows(np.arange(0, NF, STEP)) / math.sqrt(NF)).astype(np.float32)
    fine = phase_rows(np.arange(STEP)).astype(np.float32)
    bf16, f32 = jnp.bfloat16, jnp.float32
    vmem = pl.BlockSpec(memory_space=pltpu.VMEM)
    hbm = pl.BlockSpec(memory_space=pl.ANY)
    peers = nsub * nfrq
    dma = pltpu.SemaphoreType.DMA
    return pl.pallas_call(
        functools.partial(kernel, n, nsub, nfrq, chunks, pair_block, stack_block),
        out_shape=jax.ShapeDtypeStruct((SLOTS_DEV, lag_width), f32),
        in_specs=[hbm, vmem, vmem, vmem, vmem, vmem, hbm, vmem],
        out_specs=vmem,
        scratch_shapes=[
            pltpu.VMEM((128, 128), f32),
            pltpu.VMEM((pairs, 2), jnp.int32),
            pltpu.VMEM((1, pairs), jnp.int32),
            pltpu.VMEM((2, channels, bins), bf16),
            pltpu.VMEM((2, VS_BLK, 8, bins), bf16),
            pltpu.VMEM((n, chunks, 2, VS_BLK, width), bf16),
            pltpu.VMEM((2, pairs, bins), bf16),
            pltpu.VMEM((pairs, channels), bf16),
            pltpu.VMEM((stacks, pairs), bf16),
            pltpu.VMEM((pairs, 2 * width), bf16),
            pltpu.VMEM((stacks, 2 * width), bf16),
            pltpu.VMEM((chunks, 2, width, LAGS), bf16),
            pltpu.VMEM((2, bins // STEP, LAGS), f32),
            pltpu.VMEM((stacks, LAGS), f32),
            pltpu.VMEM((peers - 1, stacks, lag_width), bf16),
            pltpu.VMEM((peers - 1, stacks, lag_width), bf16),
            pltpu.VMEM((stacks, lag_width), f32),
            pltpu.VMEM((n, SLOTS_DEV, lag_width), bf16),
            pltpu.VMEM((n - 1, SLOTS_DEV, lag_width), bf16),
            dma((2 + chunks,)),
            dma((chunks, n - 1)), dma((chunks, n - 1)),
            dma((chunks, n - 1)), dma((chunks, n - 1)),
            dma((peers - 1,)), dma((peers - 1,)),
            dma((n - 1,)), dma((n - 1,)),
        ],
        compiler_params=pltpu.CompilerParams(collective_id=0, has_side_effects=True),
    )(spectra.reshape(2, VS_BLK, channels // VS_BLK, bins), channel_mask,
      local_channel, partner_channel, stack_owner.reshape(n, 1, -1), stack_slot,
      jnp.asarray(coarse), jnp.asarray(fine))


def solution(mesh):
    sizes = (mesh.shape["blk"], mesh.shape["sub"], mesh.shape["frq"])
    return jax.shard_map(
        functools.partial(per_device, sizes),
        mesh=mesh,
        in_specs=(
            P(None, ("grp", "blk"), ("sub", "frq")),
            P(("grp", "blk"), None),
            P(("grp", "blk"), None, None),
            P(("grp", "blk"), None, None),
            P(("grp", "blk"), None, None, None),
            P(("grp", "blk"), None, None),
        ),
        out_specs=P(("grp", "blk"), ("sub", "frq")),
        check_vma=False,
    )
```

```python
import functools
import math

import jax
import jax.numpy as jnp
import numpy as np
from jax import lax
from jax.experimental import pallas as pl
from jax.experimental.pallas import tpu as pltpu
from jax.sharding import PartitionSpec as P

NF = 4096
LAGS = 1024
VS_BLK = 32
SLOTS_DEV = 32
STEP = 32
MESH = pl.DeviceIdType.MESH


def phase_rows(bins):
    shifts = np.arange(LAGS, dtype=np.int64) - LAGS // 2
    angle = np.mod(bins[:, None] * shifts[None, :], NF) * (2.0 * math.pi / NF)
    return np.stack([np.cos(angle), -np.sin(angle)])


def loop(count, body):
    if count == 1:
        body(0)
    else:
        lax.fori_loop(0, count, lambda i, carry: (body(i), carry)[1], 0)


def steps(count, body):
    if count <= 8:
        for i in range(count):
            body(i)
    else:
        lax.fori_loop(0, count, lambda i, carry: (body(i), carry)[1], 0)


def kernel(n, nsub, nfrq, chunks, pair_block, stack_block,
           spectra, mask_ref, local_ref, partner_ref, owner_ref, slot_ref, coarse, fine_ref, out_ref,
           index_rows, index_cols, stack_row,
           spec, tiles, panels, own, hot, sel, cross, stacked, table, coarse_v, acc,
           send1, recv1, total, send2, recv2,
           tile_sem, load_sem, right_send, right_recv, left_send, left_recv,
           s1_send, s1_recv, s2_send, s2_recv):
    z = lax.axis_index("blk")
    sub, frq = lax.axis_index("sub"), lax.axis_index("frq")
    place = sub * nfrq + frq
    channels, bins = spec.shape[1], spec.shape[2]
    width = bins // chunks
    pairs, stacks = own.shape[1], acc.shape[0]
    lag_width = out_ref.shape[1]
    coarse_rows = bins // STEP
    peers = [(ds, df) for ds in range(nsub - 1, -1, -1) for df in range(nfrq - 1, -1, -1)]

    tile_loads = []
    for c in range(chunks):
        lanes = pl.ds(c * width, width)
        tile_loads.append(pltpu.make_async_copy(
            spectra.at[:, :, pl.ds(0, 8), lanes], tiles.at[:, :, :, lanes], tile_sem.at[c]))
    for load in tile_loads:
        load.start()
    flat = spectra.reshape(2, channels, bins)
    spec_loads = []
    for c in range(chunks):
        lanes = pl.ds(c * width, width)
        spec_loads.append(pltpu.make_async_copy(
            flat.at[:, :, lanes], spec.at[:, :, lanes], load_sem.at[1 + c]))
    coarse_load = pltpu.make_async_copy(
        coarse.at[:, pl.ds(pl.multiple_of(place * coarse_rows, 8), coarse_rows), :],
        coarse_v, load_sem.at[0])
    barrier = pltpu.get_barrier_semaphore()

    @pl.when(z + 1 < n)
    def _():
        pl.semaphore_signal(barrier, inc=1, device_id={"blk": z + 1}, device_id_type=MESH)

    @pl.when(z - 1 >= 0)
    def _():
        pl.semaphore_signal(barrier, inc=1, device_id={"blk": z - 1}, device_id_type=MESH)

    for ds, df in peers[:-1]:
        pl.semaphore_signal(
            barrier, inc=1,
            device_id={"sub": lax.rem(sub + ds, nsub), "frq": lax.rem(frq + df, nfrq)},
            device_id_type=MESH)

    mask = mask_ref[...]
    at_row = lax.broadcasted_iota(jnp.int32, (VS_BLK, channels), 0)
    at_lane = lax.broadcasted_iota(jnp.int32, (VS_BLK, channels), 1)
    source_mask = jnp.sum(
        jnp.where(at_lane == at_row * (channels // VS_BLK), mask, 0).astype(jnp.float32),
        axis=1, keepdims=True)
    pick_row = lax.broadcasted_iota(jnp.int32, (VS_BLK, 8 * VS_BLK), 0)
    pick_lane = lax.broadcasted_iota(jnp.int32, (VS_BLK, 8 * VS_BLK), 1)
    pick = jnp.where(pick_lane == 8 * pick_row, source_mask, 0.0).astype(jnp.bfloat16)
    def to_right(c, d):
        return pltpu.make_async_remote_copy(
            src_ref=panels.at[z - d, c], dst_ref=panels.at[z - d, c],
            send_sem=right_send.at[c, d], recv_sem=right_recv.at[c, d],
            device_id={"blk": z + 1}, device_id_type=MESH)

    def to_left(c, d):
        return pltpu.make_async_remote_copy(
            src_ref=panels.at[z + d, c], dst_ref=panels.at[z + d, c],
            send_sem=left_send.at[c, d], recv_sem=left_recv.at[c, d],
            device_id={"blk": z - 1}, device_id_type=MESH)

    def from_left(c, d):
        return pltpu.make_async_remote_copy(
            src_ref=panels.at[z - 1 - d, c], dst_ref=panels.at[z - 1 - d, c],
            send_sem=right_send.at[c, d], recv_sem=right_recv.at[c, d],
            device_id={"blk": z - 1}, device_id_type=MESH)

    def from_right(c, d):
        return pltpu.make_async_remote_copy(
            src_ref=panels.at[z + 1 + d, c], dst_ref=panels.at[z + 1 + d, c],
            send_sem=left_send.at[c, d], recv_sem=left_recv.at[c, d],
            device_id={"blk": z + 1}, device_id_type=MESH)

    def send_on(c, d):
        @pl.when((z - d >= 0) & (z + 1 < n))
        def _():
            to_right(c, d).start()

        @pl.when((z + d < n) & (z - 1 >= 0))
        def _():
            to_left(c, d).start()

    def arrive(c, d):
        @pl.when(z - 1 - d >= 0)
        def _():
            from_left(c, d).wait_recv()

        @pl.when(z + 1 + d < n)
        def _():
            from_right(c, d).wait_recv()

        if d + 1 < n - 1:
            send_on(c, d + 1)

    for c in range(chunks):
        tile_loads[c].wait()
        lanes = pl.ds(c * width, width)
        for part in range(2):
            panels[z, c, part] = jnp.dot(
                pick, tiles[part, :, :, lanes].reshape(8 * VS_BLK, width),
                preferred_element_type=jnp.float32).astype(jnp.bfloat16)
        if c == 0:
            ends = jnp.where(z == 0, 1, 0) + jnp.where(z == n - 1, 1, 0)
            pl.semaphore_wait(barrier, len(peers) + 1 - ends)
        send_on(c, 0)
    for load in spec_loads:
        load.start()
    coarse_load.start()

    def build_hot():
        per_panel = local_ref.shape[2]
        index_rows[...] = jnp.zeros_like(index_rows)
        index_rows[0:n, 0:per_panel] = local_ref[0].astype(jnp.float32)
        index_rows[n:2 * n, 0:per_panel] = partner_ref[0].astype(jnp.float32)
        turned = index_rows[...].T
        for p in range(n):
            rows = pl.ds(p * per_panel, per_panel)
            index_cols[rows, 0:1] = turned[0:per_panel, p:p + 1].astype(jnp.int32)
            index_cols[rows, 1:2] = turned[0:per_panel, n + p:n + p + 1].astype(jnp.int32) + p * VS_BLK
            stack_row[0:1, p * per_panel:(p + 1) * per_panel] = (
                owner_ref[p] * SLOTS_DEV + slot_ref[0, p:p + 1, :])

        def body(r):
            rows = pl.ds(pl.multiple_of(r * pair_block, 16), pair_block)
            lane = lax.broadcasted_iota(jnp.int32, (pair_block, channels), 1)
            hit = jnp.where(lane == index_cols[rows, 0:1], mask, 0)
            hot[rows, :] = hit.astype(jnp.float32).astype(jnp.bfloat16)
        loop(pairs // pair_block, body)

        def body_sel(r):
            rows = pl.ds(pl.multiple_of(r * stack_block, 16), stack_block)
            row = lax.broadcasted_iota(jnp.int32, (stack_block, pairs), 0) + r * stack_block
            hit = jnp.where(row == stack_row[0:1, :], 1.0, 0.0)
            sel[rows, :] = hit.astype(jnp.bfloat16)
        loop(stacks // stack_block, body_sel)

    def gather(c):
        spec_loads[c].wait()
        for part in range(2):
            def body(r):
                rows = pl.ds(pl.multiple_of(r * pair_block, 16), pair_block)
                lanes = pl.ds(c * width, width)
                own[part, rows, lanes] = jnp.dot(
                    hot[rows, :], spec[part, :, lanes],
                    preferred_element_type=jnp.float32).astype(jnp.bfloat16)
            loop(pairs // pair_block, body)

    def make_table(c):
        if c == 0:
            coarse_load.wait()

        def body(a):
            row = pl.ds(c * (width // STEP) + a, 1)
            high_cos, high_sin = coarse_v[0, row, :], coarse_v[1, row, :]
            low_cos, low_sin = fine_ref[0], fine_ref[1]
            rows = pl.ds(pl.multiple_of(a * STEP, STEP), STEP)
            table[c, 0, rows, :] = (high_cos * low_cos - high_sin * low_sin).astype(jnp.bfloat16)
            table[c, 1, rows, :] = (high_sin * low_cos + high_cos * low_sin).astype(jnp.bfloat16)
        loop(width // STEP, body)

    work = [functools.partial(build_hot)]
    for c in range(chunks):
        work += [functools.partial(gather, c), functools.partial(make_table, c)]
    work.pop(0)()
    work.pop(0)()

    for d in range(n - 2):
        for c in range(chunks):
            arrive(c, d)
            if work:
                work.pop(0)()
    while work:
        work.pop(0)()

    def stack_chunk(c):
        lanes = pl.ds(c * width, width)
        panel = [panels[:, c, part].reshape(n * VS_BLK, width) for part in range(2)]

        def body(r):
            rows = pl.ds(pl.multiple_of(r * pair_block, 16), pair_block)
            lane = lax.broadcasted_iota(jnp.int32, (pair_block, n * VS_BLK), 1)
            hit = jnp.where(lane == index_cols[rows, 1:2], 1.0, 0.0).astype(jnp.bfloat16)
            partner = [jnp.dot(hit, half, preferred_element_type=jnp.float32) for half in panel]
            mine = [own[part, rows, lanes].astype(jnp.float32) for part in range(2)]
            cross[rows, 0:width] = (
                mine[0] * partner[0] + mine[1] * partner[1]).astype(jnp.bfloat16)
            cross[rows, width:2 * width] = (
                mine[1] * partner[0] - mine[0] * partner[1]).astype(jnp.bfloat16)
        loop(pairs // pair_block, body)

        def body_stack(r):
            rows = pl.ds(pl.multiple_of(r * stack_block, 16), stack_block)
            stacked[rows, :] = jnp.dot(
                sel[rows, :], cross[...], preferred_element_type=jnp.float32).astype(jnp.bfloat16)
        loop(stacks // stack_block, body_stack)

    for c in range(chunks):
        arrive(c, n - 2)
        stack_chunk(c)
        if c < chunks - 1:
            def body(r):
                rows = pl.ds(pl.multiple_of(r * stack_block, 16), stack_block)
                product = jnp.dot(
                    stacked[rows, :], table[c].reshape(2 * width, LAGS),
                    preferred_element_type=jnp.float32)
                acc[rows, :] = product if c == 0 else acc[rows, :] + product
            loop(stacks // stack_block, body)

    targets = []
    last = chunks - 1

    def owner_at(j):
        return jnp.where(z < n // 2, n - 1 - j, j)

    def share_copy(k, owner):
        rows = pl.ds(pl.multiple_of(owner * SLOTS_DEV, SLOTS_DEV), SLOTS_DEV)
        return pltpu.make_async_remote_copy(
            src_ref=send1.at[k, rows, :], dst_ref=recv1.at[k, rows, :],
            send_sem=s1_send.at[k, owner], recv_sem=s1_recv.at[k, owner],
            device_id={"sub": targets[k][0], "frq": targets[k][1]}, device_id_type=MESH)

    def owner_copy(owner):
        return pltpu.make_async_remote_copy(
            src_ref=send2.at[owner], dst_ref=recv2.at[z],
            send_sem=s2_send.at[owner], recv_sem=s2_recv.at[z],
            device_id={"blk": owner}, device_id_type=MESH)

    def send_shares(ks):
        def turn(j):
            for k in ks:
                share_copy(k, owner_at(j)).start()
        steps(n, turn)

    for k, (ds, df) in enumerate(peers):
        to_sub, to_frq = lax.rem(sub + ds, nsub), lax.rem(frq + df, nfrq)
        lanes = pl.ds(pl.multiple_of((to_sub * nfrq + to_frq) * lag_width, 128), lag_width)
        own_share = k == len(peers) - 1

        def body(r):
            rows = pl.ds(pl.multiple_of(r * stack_block, 16), stack_block)
            product = jnp.dot(
                stacked[rows, :], table[last, :, :, lanes].reshape(2 * width, lag_width),
                preferred_element_type=jnp.float32)
            if last > 0:
                product = product + acc[rows, lanes]
            if own_share:
                total[rows, :] = product
            else:
                send1[k, rows, :] = product.astype(jnp.bfloat16)
        loop(stacks // stack_block, body)
        targets.append((to_sub, to_frq))
        if k == max(len(peers) - 3, 0):
            send_shares(range(k + 1))
        elif not own_share and k > len(peers) - 3:
            send_shares([k])

    def owner_turn(j):
        owner = owner_at(j)
        rows = pl.ds(pl.multiple_of(owner * SLOTS_DEV, SLOTS_DEV), SLOTS_DEV)
        summed = total[rows, :]
        for k in range(len(peers) - 1):
            share_copy(k, owner).wait_recv()
            summed = summed + recv1[k, rows, :].astype(jnp.float32)
        total[rows, :] = summed
        send2[owner] = summed.astype(jnp.bfloat16)

        @pl.when(owner != z)
        def _():
            owner_copy(owner).start()
    steps(n, owner_turn)
    result = total[pl.ds(pl.multiple_of(z * SLOTS_DEV, SLOTS_DEV), SLOTS_DEV), :]

    for c in range(chunks):
        for d in range(n - 1):
            @pl.when((z - d >= 0) & (z + 1 < n))
            def _():
                to_right(c, d).wait_send()

            @pl.when((z + d < n) & (z - 1 >= 0))
            def _():
                to_left(c, d).wait_send()
    def shares_left(j):
        for k in range(len(peers) - 1):
            share_copy(k, j).wait_send()
    steps(n, shares_left)
    out_ref[...] = result

    def add_block(k):
        source = lax.rem(z + 1 + k, n)
        pltpu.make_async_remote_copy(
            src_ref=send2.at[source], dst_ref=recv2.at[source],
            send_sem=s2_send.at[source], recv_sem=s2_recv.at[source],
            device_id={"blk": source}, device_id_type=MESH).wait_recv()
        out_ref[...] += recv2[source].astype(jnp.float32)
    steps(n - 1, add_block)
    steps(n - 1, lambda k: owner_copy(lax.rem(z + 1 + k, n)).wait_send())


def per_device(sizes, spectra, channel_mask, local_channel, partner_channel, stack_owner, stack_slot):
    n, nsub, nfrq = sizes
    channels, bins = spectra.shape[1], spectra.shape[2]
    chunks = 4 if n <= 8 else 1
    width = bins // chunks
    pairs = local_channel.shape[1] * local_channel.shape[2]
    stacks = n * SLOTS_DEV
    lag_width = LAGS // (nsub * nfrq)
    pair_block = 192 if pairs % 192 == 0 else pairs
    stack_block = 128 if stacks % 128 == 0 else stacks
    coarse = (phase_rows(np.arange(0, NF, STEP)) / math.sqrt(NF)).astype(np.float32)
    fine = phase_rows(np.arange(STEP)).astype(np.float32)
    bf16, f32 = jnp.bfloat16, jnp.float32
    vmem = pl.BlockSpec(memory_space=pltpu.VMEM)
    hbm = pl.BlockSpec(memory_space=pl.ANY)
    peers = nsub * nfrq
    dma = pltpu.SemaphoreType.DMA
    return pl.pallas_call(
        functools.partial(kernel, n, nsub, nfrq, chunks, pair_block, stack_block),
        out_shape=jax.ShapeDtypeStruct((SLOTS_DEV, lag_width), f32),
        in_specs=[hbm, vmem, vmem, vmem, vmem, vmem, hbm, vmem],
        out_specs=vmem,
        scratch_shapes=[
            pltpu.VMEM((128, 128), f32),
            pltpu.VMEM((pairs, 2), jnp.int32),
            pltpu.VMEM((1, pairs), jnp.int32),
            pltpu.VMEM((2, channels, bins), bf16),
            pltpu.VMEM((2, VS_BLK, 8, bins), bf16),
            pltpu.VMEM((n, chunks, 2, VS_BLK, width), bf16),
            pltpu.VMEM((2, pairs, bins), bf16),
            pltpu.VMEM((pairs, channels), bf16),
            pltpu.VMEM((stacks, pairs), bf16),
            pltpu.VMEM((pairs, 2 * width), bf16),
            pltpu.VMEM((stacks, 2 * width), bf16),
            pltpu.VMEM((chunks, 2, width, LAGS), bf16),
            pltpu.VMEM((2, bins // STEP, LAGS), f32),
            pltpu.VMEM((stacks, LAGS), f32),
            pltpu.VMEM((peers - 1, stacks, lag_width), bf16),
            pltpu.VMEM((peers - 1, stacks, lag_width), bf16),
            pltpu.VMEM((stacks, lag_width), f32),
            pltpu.VMEM((n, SLOTS_DEV, lag_width), bf16),
            pltpu.VMEM((n, SLOTS_DEV, lag_width), bf16),
            dma((chunks,)), dma((1 + chunks,)),
            dma((chunks, n - 1)), dma((chunks, n - 1)),
            dma((chunks, n - 1)), dma((chunks, n - 1)),
            dma((peers - 1, n)), dma((peers - 1, n)),
            dma((n,)), dma((n,)),
        ],
        compiler_params=pltpu.CompilerParams(collective_id=0, has_side_effects=True),
    )(spectra.reshape(2, VS_BLK, channels // VS_BLK, bins), channel_mask,
      local_channel, partner_channel, stack_owner.reshape(n, 1, -1), stack_slot,
      jnp.asarray(coarse), jnp.asarray(fine))


def solution(mesh):
    sizes = (mesh.shape["blk"], mesh.shape["sub"], mesh.shape["frq"])
    return jax.shard_map(
        functools.partial(per_device, sizes),
        mesh=mesh,
        in_specs=(
            P(None, ("grp", "blk"), ("sub", "frq")),
            P(("grp", "blk"), None),
            P(("grp", "blk"), None, None),
            P(("grp", "blk"), None, None),
            P(("grp", "blk"), None, None, None),
            P(("grp", "blk"), None, None),
        ),
        out_specs=P(("grp", "blk"), ("sub", "frq")),
        check_vma=False,
    )
```

```python
import functools
import math

import jax
import jax.numpy as jnp
import numpy as np
from jax import lax
from jax.experimental import pallas as pl
from jax.experimental.pallas import tpu as pltpu
from jax.sharding import PartitionSpec as P

NF = 4096
LAGS = 1024
VS_BLK = 32
SLOTS_DEV = 32
STEP = 32
MESH = pl.DeviceIdType.MESH


def phase_rows(bins):
    shifts = np.arange(LAGS, dtype=np.int64) - LAGS // 2
    angle = np.mod(bins[:, None] * shifts[None, :], NF) * (2.0 * math.pi / NF)
    return np.stack([np.cos(angle), -np.sin(angle)])


def loop(count, body):
    if count == 1:
        body(0)
    else:
        lax.fori_loop(0, count, lambda i, carry: (body(i), carry)[1], 0)


def steps(count, body):
    if count <= 8:
        for i in range(count):
            body(i)
    else:
        lax.fori_loop(0, count, lambda i, carry: (body(i), carry)[1], 0)


def kernel(n, nsub, nfrq, chunks, pair_block, stack_block,
           spectra, mask_hbm, local_hbm, partner_hbm, owner_hbm, slot_hbm, coarse, fine_hbm, out_ref,
           mask_ref, local_ref, partner_ref, owner_ref, slot_ref, fine_ref,
           index_rows, index_cols, stack_row,
           spec, tiles, panels, own, hot, sel, cross, stacked, table, coarse_v, acc,
           send1, recv1, total, send2, recv2,
           list_sem, tile_sem, load_sem, right_send, right_recv, left_send, left_recv,
           s1_send, s1_recv, s2_send, s2_recv):
    z = lax.axis_index("blk")
    sub, frq = lax.axis_index("sub"), lax.axis_index("frq")
    place = sub * nfrq + frq
    channels, bins = spec.shape[1], spec.shape[2]
    width = bins // chunks
    pairs, stacks = own.shape[1], acc.shape[0]
    lag_width = out_ref.shape[2]
    coarse_rows = bins // STEP
    peers = [(ds, df) for ds in range(nsub - 1, -1, -1) for df in range(nfrq - 1, -1, -1)]

    barrier = pltpu.get_barrier_semaphore()

    @pl.when(z + 1 < n)
    def _():
        pl.semaphore_signal(barrier, inc=1, device_id={"blk": z + 1}, device_id_type=MESH)

    @pl.when(z - 1 >= 0)
    def _():
        pl.semaphore_signal(barrier, inc=1, device_id={"blk": z - 1}, device_id_type=MESH)

    for ds, df in peers[:-1]:
        pl.semaphore_signal(
            barrier, inc=1,
            device_id={"sub": lax.rem(sub + ds, nsub), "frq": lax.rem(frq + df, nfrq)},
            device_id_type=MESH)

    list_loads = [
        pltpu.make_async_copy(far, near, list_sem.at[i])
        for i, (far, near) in enumerate([
            (mask_hbm, mask_ref), (local_hbm, local_ref), (partner_hbm, partner_ref),
            (owner_hbm, owner_ref), (slot_hbm, slot_ref), (fine_hbm, fine_ref)])]
    list_loads[0].start()
    tile_loads = []
    for c in range(chunks):
        lanes = pl.ds(c * width, width)
        tile_loads.append(pltpu.make_async_copy(
            spectra.at[:, :, pl.ds(0, 8), lanes], tiles.at[:, :, :, lanes], tile_sem.at[c]))
    for load in tile_loads:
        load.start()
    for load in list_loads[1:5]:
        load.start()
    flat = spectra.reshape(2, channels, bins)
    spec_loads = []
    for c in range(chunks):
        lanes = pl.ds(c * width, width)
        spec_loads.append(pltpu.make_async_copy(
            flat.at[:, :, lanes], spec.at[:, :, lanes], load_sem.at[1 + c]))
    coarse_load = pltpu.make_async_copy(
        coarse.at[:, pl.ds(pl.multiple_of(place * coarse_rows, 8), coarse_rows), :],
        coarse_v, load_sem.at[0])
    list_loads[0].wait()
    mask = mask_ref[...]
    at_row = lax.broadcasted_iota(jnp.int32, (VS_BLK, channels), 0)
    at_lane = lax.broadcasted_iota(jnp.int32, (VS_BLK, channels), 1)
    source_mask = jnp.sum(
        jnp.where(at_lane == at_row * (channels // VS_BLK), mask, 0).astype(jnp.float32),
        axis=1, keepdims=True)
    pick_row = lax.broadcasted_iota(jnp.int32, (VS_BLK, 8 * VS_BLK), 0)
    pick_lane = lax.broadcasted_iota(jnp.int32, (VS_BLK, 8 * VS_BLK), 1)
    pick = jnp.where(pick_lane == 8 * pick_row, source_mask, 0.0).astype(jnp.bfloat16)
    def to_right(c, d):
        return pltpu.make_async_remote_copy(
            src_ref=panels.at[z - d, c], dst_ref=panels.at[z - d, c],
            send_sem=right_send.at[c, d], recv_sem=right_recv.at[c, d],
            device_id={"blk": z + 1}, device_id_type=MESH)

    def to_left(c, d):
        return pltpu.make_async_remote_copy(
            src_ref=panels.at[z + d, c], dst_ref=panels.at[z + d, c],
            send_sem=left_send.at[c, d], recv_sem=left_recv.at[c, d],
            device_id={"blk": z - 1}, device_id_type=MESH)

    def from_left(c, d):
        return pltpu.make_async_remote_copy(
            src_ref=panels.at[z - 1 - d, c], dst_ref=panels.at[z - 1 - d, c],
            send_sem=right_send.at[c, d], recv_sem=right_recv.at[c, d],
            device_id={"blk": z - 1}, device_id_type=MESH)

    def from_right(c, d):
        return pltpu.make_async_remote_copy(
            src_ref=panels.at[z + 1 + d, c], dst_ref=panels.at[z + 1 + d, c],
            send_sem=left_send.at[c, d], recv_sem=left_recv.at[c, d],
            device_id={"blk": z + 1}, device_id_type=MESH)

    def send_on(c, d):
        @pl.when((z - d >= 0) & (z + 1 < n))
        def _():
            to_right(c, d).start()

        @pl.when((z + d < n) & (z - 1 >= 0))
        def _():
            to_left(c, d).start()

    def arrive(c, d):
        @pl.when(z - 1 - d >= 0)
        def _():
            from_left(c, d).wait_recv()

        @pl.when(z + 1 + d < n)
        def _():
            from_right(c, d).wait_recv()

        if d + 1 < n - 1:
            send_on(c, d + 1)

    for c in range(chunks):
        tile_loads[c].wait()
        lanes = pl.ds(c * width, width)
        for part in range(2):
            panels[z, c, part] = jnp.dot(
                pick, tiles[part, :, :, lanes].reshape(8 * VS_BLK, width),
                preferred_element_type=jnp.float32).astype(jnp.bfloat16)
        if c == 0:
            ends = jnp.where(z == 0, 1, 0) + jnp.where(z == n - 1, 1, 0)
            pl.semaphore_wait(barrier, len(peers) + 1 - ends)
        send_on(c, 0)
    for load in spec_loads:
        load.start()
    coarse_load.start()
    list_loads[5].start()

    def build_hot():
        for load in list_loads[1:5]:
            load.wait()
        per_panel = local_ref.shape[2]
        index_rows[...] = jnp.zeros_like(index_rows)
        index_rows[0:n, 0:per_panel] = local_ref[0].astype(jnp.float32)
        index_rows[n:2 * n, 0:per_panel] = partner_ref[0].astype(jnp.float32)
        turned = index_rows[...].T
        for p in range(n):
            rows = pl.ds(p * per_panel, per_panel)
            index_cols[rows, 0:1] = turned[0:per_panel, p:p + 1].astype(jnp.int32)
            index_cols[rows, 1:2] = turned[0:per_panel, n + p:n + p + 1].astype(jnp.int32) + p * VS_BLK
            stack_row[0:1, p * per_panel:(p + 1) * per_panel] = (
                owner_ref[p] * SLOTS_DEV + slot_ref[0, p:p + 1, :])

        def body(r):
            rows = pl.ds(pl.multiple_of(r * pair_block, 16), pair_block)
            lane = lax.broadcasted_iota(jnp.int32, (pair_block, channels), 1)
            hit = jnp.where(lane == index_cols[rows, 0:1], mask, 0)
            hot[rows, :] = hit.astype(jnp.float32).astype(jnp.bfloat16)
        loop(pairs // pair_block, body)

        def body_sel(r):
            rows = pl.ds(pl.multiple_of(r * stack_block, 16), stack_block)
            row = lax.broadcasted_iota(jnp.int32, (stack_block, pairs), 0) + r * stack_block
            hit = jnp.where(row == stack_row[0:1, :], 1.0, 0.0)
            sel[rows, :] = hit.astype(jnp.bfloat16)
        loop(stacks // stack_block, body_sel)

    def gather(c):
        spec_loads[c].wait()
        for part in range(2):
            def body(r):
                rows = pl.ds(pl.multiple_of(r * pair_block, 16), pair_block)
                lanes = pl.ds(c * width, width)
                own[part, rows, lanes] = jnp.dot(
                    hot[rows, :], spec[part, :, lanes],
                    preferred_element_type=jnp.float32).astype(jnp.bfloat16)
            loop(pairs // pair_block, body)

    def make_table(c):
        if c == 0:
            coarse_load.wait()
            list_loads[5].wait()

        def body(a):
            row = pl.ds(c * (width // STEP) + a, 1)
            high_cos, high_sin = coarse_v[0, row, :], coarse_v[1, row, :]
            low_cos, low_sin = fine_ref[0], fine_ref[1]
            rows = pl.ds(pl.multiple_of(a * STEP, STEP), STEP)
            table[c, 0, rows, :] = (high_cos * low_cos - high_sin * low_sin).astype(jnp.bfloat16)
            table[c, 1, rows, :] = (high_sin * low_cos + high_cos * low_sin).astype(jnp.bfloat16)
        loop(width // STEP, body)

    work = [functools.partial(build_hot)]
    for c in range(chunks):
        work += [functools.partial(gather, c), functools.partial(make_table, c)]
    work.pop(0)()
    work.pop(0)()

    for d in range(n - 2):
        for c in range(chunks):
            arrive(c, d)
            if work:
                work.pop(0)()
    while work:
        work.pop(0)()

    def stack_chunk(c):
        lanes = pl.ds(c * width, width)
        panel = [panels[:, c, part].reshape(n * VS_BLK, width) for part in range(2)]

        def body(r):
            rows = pl.ds(pl.multiple_of(r * pair_block, 16), pair_block)
            lane = lax.broadcasted_iota(jnp.int32, (pair_block, n * VS_BLK), 1)
            hit = jnp.where(lane == index_cols[rows, 1:2], 1.0, 0.0).astype(jnp.bfloat16)
            partner = [jnp.dot(hit, half, preferred_element_type=jnp.float32) for half in panel]
            mine = [own[part, rows, lanes].astype(jnp.float32) for part in range(2)]
            cross[rows, 0:width] = (
                mine[0] * partner[0] + mine[1] * partner[1]).astype(jnp.bfloat16)
            cross[rows, width:2 * width] = (
                mine[1] * partner[0] - mine[0] * partner[1]).astype(jnp.bfloat16)
        loop(pairs // pair_block, body)

        def body_stack(r):
            rows = pl.ds(pl.multiple_of(r * stack_block, 16), stack_block)
            stacked[rows, :] = jnp.dot(
                sel[rows, :], cross[...], preferred_element_type=jnp.float32).astype(jnp.bfloat16)
        loop(stacks // stack_block, body_stack)

    for c in range(chunks):
        arrive(c, n - 2)
        stack_chunk(c)
        if c < chunks - 1:
            def body(r):
                rows = pl.ds(pl.multiple_of(r * stack_block, 16), stack_block)
                product = jnp.dot(
                    stacked[rows, :], table[c].reshape(2 * width, LAGS),
                    preferred_element_type=jnp.float32)
                acc[rows, :] = product if c == 0 else acc[rows, :] + product
            loop(stacks // stack_block, body)

    targets = []
    last = chunks - 1

    def owner_at(j):
        return jnp.where(z < n // 2, n - 1 - j, j)

    def share_copy(k, owner):
        rows = pl.ds(pl.multiple_of(owner * SLOTS_DEV, SLOTS_DEV), SLOTS_DEV)
        return pltpu.make_async_remote_copy(
            src_ref=send1.at[k, rows, :], dst_ref=recv1.at[k, rows, :],
            send_sem=s1_send.at[k, owner], recv_sem=s1_recv.at[k, owner],
            device_id={"sub": targets[k][0], "frq": targets[k][1]}, device_id_type=MESH)

    def owner_copy(owner):
        return pltpu.make_async_remote_copy(
            src_ref=send2.at[owner], dst_ref=recv2.at[z],
            send_sem=s2_send.at[owner], recv_sem=s2_recv.at[z],
            device_id={"blk": owner}, device_id_type=MESH)

    def send_shares(ks):
        def turn(j):
            for k in ks:
                share_copy(k, owner_at(j)).start()
        steps(n, turn)

    for k, (ds, df) in enumerate(peers):
        to_sub, to_frq = lax.rem(sub + ds, nsub), lax.rem(frq + df, nfrq)
        lanes = pl.ds(pl.multiple_of((to_sub * nfrq + to_frq) * lag_width, 128), lag_width)
        own_share = k == len(peers) - 1

        def body(r):
            rows = pl.ds(pl.multiple_of(r * stack_block, 16), stack_block)
            product = jnp.dot(
                stacked[rows, :], table[last, :, :, lanes].reshape(2 * width, lag_width),
                preferred_element_type=jnp.float32)
            if last > 0:
                product = product + acc[rows, lanes]
            if own_share:
                total[rows, :] = product
            else:
                send1[k, rows, :] = product.astype(jnp.bfloat16)
        loop(stacks // stack_block, body)
        targets.append((to_sub, to_frq))
        if k == max(len(peers) - 3, 0):
            send_shares(range(k + 1))
        elif not own_share and k > len(peers) - 3:
            send_shares([k])

    def owner_turn(j):
        owner = owner_at(j)
        rows = pl.ds(pl.multiple_of(owner * SLOTS_DEV, SLOTS_DEV), SLOTS_DEV)
        summed = total[rows, :]
        for k in range(len(peers) - 1):
            share_copy(k, owner).wait_recv()
            summed = summed + recv1[k, rows, :].astype(jnp.float32)
        total[rows, :] = summed
        send2[owner] = summed.astype(jnp.bfloat16)

        @pl.when(owner != z)
        def _():
            owner_copy(owner).start()
    steps(n, owner_turn)
    result = total[pl.ds(pl.multiple_of(z * SLOTS_DEV, SLOTS_DEV), SLOTS_DEV), :]

    for c in range(chunks):
        for d in range(n - 1):
            @pl.when((z - d >= 0) & (z + 1 < n))
            def _():
                to_right(c, d).wait_send()

            @pl.when((z + d < n) & (z - 1 >= 0))
            def _():
                to_left(c, d).wait_send()
    def shares_left(j):
        for k in range(len(peers) - 1):
            share_copy(k, j).wait_send()
    steps(n, shares_left)
    out_ref[0] = result

    def add_block(keep, k):
        source = lax.rem(z + 1 + k, n)
        pltpu.make_async_remote_copy(
            src_ref=send2.at[source], dst_ref=recv2.at[source],
            send_sem=s2_send.at[source], recv_sem=s2_recv.at[source],
            device_id={"blk": source}, device_id_type=MESH).wait_recv()
        term = recv2[source].astype(jnp.float32)
        if keep:
            out_ref[1] = term
        else:
            out_ref[0] += term
    steps(n - 2, functools.partial(add_block, False))
    add_block(True, n - 2)
    steps(n - 1, lambda k: owner_copy(lax.rem(z + 1 + k, n)).wait_send())


def per_device(sizes, spectra, channel_mask, local_channel, partner_channel, stack_owner, stack_slot):
    n, nsub, nfrq = sizes
    channels, bins = spectra.shape[1], spectra.shape[2]
    chunks = 4 if n <= 8 else 1
    width = bins // chunks
    pairs = local_channel.shape[1] * local_channel.shape[2]
    stacks = n * SLOTS_DEV
    lag_width = LAGS // (nsub * nfrq)
    pair_block = 192 if pairs % 192 == 0 else pairs
    stack_block = 128 if stacks % 128 == 0 else stacks
    coarse = (phase_rows(np.arange(0, NF, STEP)) / math.sqrt(NF)).astype(np.float32)
    fine = phase_rows(np.arange(STEP)).astype(np.float32)
    bf16, f32 = jnp.bfloat16, jnp.float32
    vmem = pl.BlockSpec(memory_space=pltpu.VMEM)
    hbm = pl.BlockSpec(memory_space=pl.ANY)
    peers = nsub * nfrq
    dma = pltpu.SemaphoreType.DMA
    halves = pl.pallas_call(
        functools.partial(kernel, n, nsub, nfrq, chunks, pair_block, stack_block),
        out_shape=jax.ShapeDtypeStruct((2, SLOTS_DEV, lag_width), f32),
        in_specs=[hbm] * 8,
        out_specs=vmem,
        scratch_shapes=[
            pltpu.VMEM(channel_mask.shape, jnp.int32),
            pltpu.VMEM(local_channel.shape, jnp.int32),
            pltpu.VMEM(partner_channel.shape, jnp.int32),
            pltpu.VMEM((n, 1, local_channel.shape[2]), jnp.int32),
            pltpu.VMEM(stack_slot.shape, jnp.int32),
            pltpu.VMEM((2, STEP, LAGS), f32),
            pltpu.VMEM((128, 128), f32),
            pltpu.VMEM((pairs, 2), jnp.int32),
            pltpu.VMEM((1, pairs), jnp.int32),
            pltpu.VMEM((2, channels, bins), bf16),
            pltpu.VMEM((2, VS_BLK, 8, bins), bf16),
            pltpu.VMEM((n, chunks, 2, VS_BLK, width), bf16),
            pltpu.VMEM((2, pairs, bins), bf16),
            pltpu.VMEM((pairs, channels), bf16),
            pltpu.VMEM((stacks, pairs), bf16),
            pltpu.VMEM((pairs, 2 * width), bf16),
            pltpu.VMEM((stacks, 2 * width), bf16),
            pltpu.VMEM((chunks, 2, width, LAGS), bf16),
            pltpu.VMEM((2, bins // STEP, LAGS), f32),
            pltpu.VMEM((stacks, LAGS), f32),
            pltpu.VMEM((peers - 1, stacks, lag_width), bf16),
            pltpu.VMEM((peers - 1, stacks, lag_width), bf16),
            pltpu.VMEM((stacks, lag_width), f32),
            pltpu.VMEM((n, SLOTS_DEV, lag_width), bf16),
            pltpu.VMEM((n, SLOTS_DEV, lag_width), bf16),
            dma((6,)), dma((chunks,)), dma((1 + chunks,)),
            dma((chunks, n - 1)), dma((chunks, n - 1)),
            dma((chunks, n - 1)), dma((chunks, n - 1)),
            dma((peers - 1, n)), dma((peers - 1, n)),
            dma((n,)), dma((n,)),
        ],
        compiler_params=pltpu.CompilerParams(collective_id=0, has_side_effects=True),
    )(spectra.reshape(2, VS_BLK, channels // VS_BLK, bins), channel_mask,
      local_channel, partner_channel, stack_owner.reshape(n, 1, -1), stack_slot,
      jnp.asarray(coarse), jnp.asarray(fine))
    return halves[0] + halves[1]


def solution(mesh):
    sizes = (mesh.shape["blk"], mesh.shape["sub"], mesh.shape["frq"])
    return jax.shard_map(
        functools.partial(per_device, sizes),
        mesh=mesh,
        in_specs=(
            P(None, ("grp", "blk"), ("sub", "frq")),
            P(("grp", "blk"), None),
            P(("grp", "blk"), None, None),
            P(("grp", "blk"), None, None),
            P(("grp", "blk"), None, None, None),
            P(("grp", "blk"), None, None),
        ),
        out_specs=P(("grp", "blk"), ("sub", "frq")),
        check_vma=False,
    )
```
